32 devices in a mesh: enc: 2 (over y), ctx: 4 (over z), tp: 4 (over x, core).
Axes of the slice: x: 2, y: 2, z: 4, core: 2. Of those that a mesh axis runs over, the one named last changes fastest.
Arguments:
- query_rows: bfloat16 [6144, 6144], P(('enc', 'ctx', 'tp')), may hold values from -5 to 5
- key_rows: bfloat16 [6144, 6144], P(('enc', 'ctx', 'tp')), may hold values from -5 to 5
- value_rows: bfloat16 [6144, 6144], P(('enc', 'ctx', 'tp')), may hold values from -6 to 6
- out_grad: bfloat16 [6144, 6144], P(('enc', 'ctx', 'tp')), may hold values from -6 to 6
- clip_lengths: int32 [16], replicated, may hold values from 1 to 768, 6144 in all
Outputs:
- attended: bfloat16 [6144, 6144], P(('enc', 'ctx', 'tp'))
- query_grad: bfloat16 [6144, 6144], P(('enc', 'ctx', 'tp'))
- key_grad: bfloat16 [6144, 6144], P(('enc', 'ctx', 'tp'))
- value_grad: bfloat16 [6144, 6144], P(('enc', 'ctx', 'tp'))
The draws below stay inside these ranges and needn't reach their ends.
Inputs may be any that keep to these rules, and one draw needn't show every extreme that they name: `clip_lengths`: clip lengths sum to 6144; the longest clip has exactly 768 tokens.
All inputs are finite; a program needn't handle non-finite values.
Results may differ from the reference program's by a relative error of at most 0.011.
Values may be sent and summed in bfloat16 or wider, within the bound.
A program may use at most 192 MiB of HBM per device.

```python
import math
import jax
import jax.numpy as jnp
import numpy as np
from jax import lax

DH = 128
ROWS = 768
F = 6144
LEN = 6144
CLIPS = 16


def draw_query_rows(key, part):
    drawn = jax.random.normal(jax.random.fold_in(key, 1), (LEN, F), jnp.float32)
    return jnp.clip(drawn, -5.0, 5.0).astype(jnp.bfloat16)


def draw_key_rows(key, part):
    drawn = jax.random.normal(jax.random.fold_in(key, 3), (LEN, F), jnp.float32)
    return jnp.clip(drawn, -5.0, 5.0).astype(jnp.bfloat16)


def level_of(key, extent, pieces, smallest, largest):
    def one(dim, parts):
        draws = jax.random.uniform(jax.random.fold_in(jax.random.fold_in(key, 6), dim), (parts,), jnp.float32, smallest / len(pieces), largest / len(pieces))
        return jnp.repeat(jnp.exp(draws), extent[dim] // parts).reshape((-1,) + (1,) * (len(extent) - dim - 1))

    factor_of = one(*pieces[0])
    for cut in pieces[1:]:
        factor_of = factor_of * one(*cut)
    return factor_of


def split_up(number_of, total, limit, skew):
    loads = [(1 << 20) // math.isqrt(grade ** skew) + 1 for grade in range(2, number_of + 1)]
    surplus, counts = total - limit - (number_of - 1), [1] * (number_of - 1)
    while surplus > 0:
        free = [i for i in range(number_of - 1) if counts[i] < limit]
        whole, remaining = sum([loads[i] for i in free]), surplus
        for i in free:
            more = min(limit - counts[i], max(1, remaining * loads[i] // whole), surplus)
            counts[i] = counts[i] + more
            surplus = surplus - more
    return np.array([limit] + counts)


def uneven_parts(rng, count, total, bound, lean):
    if count == 2:
        one = jax.random.randint(rng, (), max(1, total - bound), min(bound, total - 1) + 1)
        return jnp.stack([one, total - one])
    sizes = jnp.asarray(split_up(count, total, bound, lean), jnp.int32)
    twos = (count - 1) // 2
    source_of, receiver = sizes[1:1 + 2 * twos:2], sizes[2:2 + 2 * twos:2]
    slack = jnp.minimum(source_of - 1, bound - receiver)
    passed = jax.random.randint(jax.random.fold_in(rng, 1), (twos,), 0, 1 << 20) % (slack + 1)
    sizes = sizes.at[1:1 + 2 * twos:2].set(source_of - passed).at[2:2 + 2 * twos:2].set(receiver + passed)
    return sizes[jax.random.permutation(jax.random.fold_in(rng, 2), count)]


def normal_values(stream_key, dims, scale, limit, shards=(), kind=jnp.bfloat16):
    factor_of = level_of(stream_key, dims, shards, -0.22, 0.18) if shards else 1.0
    values = jax.random.normal(stream_key, dims, jnp.float32) * scale * factor_of
    return jnp.minimum(jnp.maximum(values, -limit), limit).astype(kind)


def setup_inputs(seed: int = 0) -> dict:
    key_of = jax.random.split(jax.random.key(seed), 6)
    return {
        "query_rows": draw_query_rows(jax.random.fold_in(key_of[5], 71), 0),
        "key_rows": draw_key_rows(jax.random.fold_in(key_of[5], 71), 0),
        "value_rows": normal_values(key_of[2], (LEN, F), 1.0, 6.0, ((0, 32),)),
        "out_grad": normal_values(key_of[3], (LEN, F), 1.0, 6.0, ((0, 32),)),
        "clip_lengths": uneven_parts(key_of[4], CLIPS, LEN, ROWS, 2).astype(jnp.int32),
    }


masked_score = -1.0e30


def clip_numbers(positions, clip_lengths):
    clip_ends = jnp.cumsum(clip_lengths).astype(jnp.int32)
    return jnp.sum((positions[:, None] >= clip_ends[None, :]).astype(jnp.int32), axis=1).astype(jnp.int32)


def window_pass(query_block, grad_block, key_window, value_window, allowed, score_scale):
    query_float = query_block.astype(jnp.float32)
    grad_float = grad_block.astype(jnp.float32)
    key_float = key_window.astype(jnp.float32)
    value_float = value_window.astype(jnp.float32)
    scores = jnp.einsum("ihd,jhd->hij", query_float, key_float) * score_scale
    scores = jnp.where(allowed[None], scores, masked_score)
    top_score = jnp.max(scores, axis=2, keepdims=True)
    log_total = top_score + jnp.log(jnp.sum(jnp.exp(scores - top_score), axis=2, keepdims=True))
    prob_float = jnp.where(allowed[None], jnp.exp(scores - log_total), 0.0)
    prob_half = lax.optimization_barrier(prob_float.astype(jnp.bfloat16)).astype(jnp.float32)
    out_float = jnp.einsum("hij,jhd->ihd", prob_half, value_float)
    correction = jnp.einsum("ihd,ihd->hi", grad_float, out_float)
    grad_prob = jnp.einsum("ihd,jhd->hij", grad_float, value_float)
    grad_score = (prob_float * (grad_prob - correction[:, :, None]) * score_scale).astype(jnp.bfloat16)
    grad_score = lax.optimization_barrier(grad_score).astype(jnp.float32)
    query_part = jnp.einsum("hij,jhd->ihd", grad_score, key_float).astype(jnp.bfloat16)
    key_part = jnp.einsum("hij,ihd->jhd", grad_score, query_float)
    value_part = jnp.einsum("hij,ihd->jhd", prob_half, grad_float)
    return out_float.astype(jnp.bfloat16), query_part, key_part, value_part


def reference(query_rows, key_rows, value_rows, out_grad, clip_lengths):
    head_count = F // DH
    head_shape = (LEN, head_count, DH)
    query_heads = query_rows.reshape(head_shape)
    grad_heads = out_grad.reshape(head_shape)
    padding = ((ROWS, ROWS), (0, 0), (0, 0))
    key_padded = jnp.pad(key_rows.reshape(head_shape), padding)
    value_padded = jnp.pad(value_rows.reshape(head_shape), padding)
    positions = jnp.arange(LEN + 2 * ROWS, dtype=jnp.int32) - ROWS
    clip_ids = clip_numbers(positions, clip_lengths)
    inside = (positions >= 0) & (positions < LEN)
    score_scale = DH ** -0.5

    def advance(carried, block_index):
        key_sum, value_sum = carried
        offset = (block_index * ROWS).astype(jnp.int32)
        query_block = lax.dynamic_slice_in_dim(query_heads, offset, ROWS, 0)
        grad_block = lax.dynamic_slice_in_dim(grad_heads, offset, ROWS, 0)
        key_window = lax.dynamic_slice_in_dim(key_padded, offset, 3 * ROWS, 0)
        value_window = lax.dynamic_slice_in_dim(value_padded, offset, 3 * ROWS, 0)
        window_ids = lax.dynamic_slice_in_dim(clip_ids, offset, 3 * ROWS, 0)
        window_inside = lax.dynamic_slice_in_dim(inside, offset, 3 * ROWS, 0)
        block_ids = lax.dynamic_slice_in_dim(clip_ids, offset + ROWS, ROWS, 0)
        allowed = (block_ids[:, None] == window_ids[None, :]) & window_inside[None, :]
        out_part, query_part, key_part, value_part = window_pass(query_block, grad_block, key_window, value_window, allowed, score_scale)
        key_sum = lax.dynamic_update_slice_in_dim(key_sum, lax.dynamic_slice_in_dim(key_sum, offset, 3 * ROWS, 0) + key_part, offset, 0)
        value_sum = lax.dynamic_update_slice_in_dim(value_sum, lax.dynamic_slice_in_dim(value_sum, offset, 3 * ROWS, 0) + value_part, offset, 0)
        return (key_sum, value_sum), (out_part, query_part)

    zeros = jnp.zeros((LEN + 2 * ROWS, head_count, DH), jnp.float32)
    (key_sum, value_sum), (outputs, query_parts) = lax.scan(advance, (zeros, zeros), jnp.arange(LEN // ROWS, dtype=jnp.int32))
    attended = outputs.reshape(LEN, F)
    query_grad = query_parts.reshape(LEN, F)
    key_grad = key_sum[ROWS:ROWS + LEN].astype(jnp.bfloat16).reshape(LEN, F)
    value_grad = value_sum[ROWS:ROWS + LEN].astype(jnp.bfloat16).reshape(LEN, F)
    return (attended, query_grad, key_grad, value_grad)
```

```python
import functools
import math

import jax
import jax.numpy as jnp
from jax import lax
from jax.experimental import pallas as pl
from jax.experimental.pallas import tpu as pltpu
from jax.sharding import PartitionSpec as P

DH = 128
GROUPS = 3
TILE = 256
ALIGN = 128
MASKED = -1e30


def widths(window):
    steps = sorted({min(w, window) for w in (256, 512, 768, 1024, window)})
    return tuple(steps)


def attention_kernel(
    plan_ref, low_ref, own_ref, high_ref, row_ids, key_ids,
    low_out, own_out, high_out,
    q_win, k_win, v_win, g_win, out_win, dq_win, dk_win, dv_win,
):
    block = pl.program_id(0)
    rows = own_ref.shape[3]
    pieces = [(low_ref, t) for t in range(low_ref.shape[1])]
    pieces += [(own_ref, t) for t in range(own_ref.shape[1])]
    pieces += [(high_ref, t) for t in range(high_ref.shape[1])]
    window = q_win.shape[0]
    for n, (ref, t) in enumerate(pieces):
        for a, win in enumerate((q_win, k_win, v_win, g_win)):
            win[pl.ds(n * rows, rows), :] = ref[0, t, a]
    dk_win[...] = jnp.zeros_like(dk_win)
    dv_win[...] = jnp.zeros_like(dv_win)
    tiles = window // TILE
    scale = DH ** -0.5
    log_scale = scale * math.log2(math.e)

    def work(i, start, width):
        here = pl.ds(pl.multiple_of(i * TILE, TILE), TILE)
        keys = pl.ds(pl.multiple_of(start, ALIGN), width)
        q, g = q_win[here, :], g_win[here, :]
        k, v = k_win[keys, :], v_win[keys, :]
        allowed = row_ids[0, here, :] == key_ids[0, :, keys]
        across = (((1,), (1,)), ((), ()))
        down = (((0,), (0,)), ((), ()))
        s = lax.dot_general(q, k, across, preferred_element_type=jnp.float32)
        s = jnp.where(allowed, s * log_scale, MASKED)
        top = jnp.maximum(jnp.max(s, axis=1, keepdims=True), 0.1 * MASKED)
        e = jnp.exp2(s - top)
        total = jnp.sum(e, axis=1, keepdims=True)
        p = e * (1.0 / jnp.where(total > 0.0, total, 1.0))
        half = p.astype(jnp.bfloat16)
        out = jnp.dot(half, v, preferred_element_type=jnp.float32)
        correction = jnp.sum(g.astype(jnp.float32) * out, axis=1, keepdims=True)
        gp = lax.dot_general(g, v, across, preferred_element_type=jnp.float32)
        ds = (p * (gp - correction)).astype(jnp.bfloat16)
        dq = jnp.dot(ds, k, preferred_element_type=jnp.float32) * scale
        out_win[here, :] = out.astype(jnp.bfloat16)
        dq_win[here, :] = dq.astype(jnp.bfloat16)
        dk_win[keys, :] += lax.dot_general(ds, q, down, preferred_element_type=jnp.float32)
        dv_win[keys, :] += lax.dot_general(half, g, down, preferred_element_type=jnp.float32)

    def one_tile(i, carry):
        start = plan_ref[block, 0, i]
        kind = plan_ref[block, 1, i]
        for n, width in enumerate(widths(window)):
            pl.when(kind == n + 1)(functools.partial(work, i, start, width))
        return carry

    lax.fori_loop(0, tiles, one_tile, 0)
    targets = [(low_out, t) for t in range(low_ref.shape[1])]
    targets += [(own_out, t) for t in range(own_ref.shape[1])]
    targets += [(high_out, t) for t in range(high_ref.shape[1])]
    for n, (ref, t) in enumerate(targets):
        part = pl.ds(n * rows, rows)
        ref[0, t, 0] = out_win[part, :]
        ref[0, t, 1] = dq_win[part, :]
        ref[0, t, 2] = (dk_win[part, :] * scale).astype(jnp.bfloat16)
        ref[0, t, 3] = dv_win[part, :].astype(jnp.bfloat16)


def attention(plan, low, own, high, row_ids, key_ids):
    blocks, parts, arrays, rows, features = own.shape
    side = low.shape[1]
    window = (parts + 2 * side) * rows
    heads = features // DH

    def spec(count):
        return pl.BlockSpec((1, count, arrays, rows, DH), lambda e, h, plan: (e, 0, 0, 0, h))

    grid_spec = pltpu.PrefetchScalarGridSpec(
        num_scalar_prefetch=1,
        grid=(blocks, heads),
        in_specs=[
            spec(side),
            spec(parts),
            spec(side),
            pl.BlockSpec((1, window, 1), lambda e, h, plan: (e, 0, 0)),
            pl.BlockSpec((1, 1, window), lambda e, h, plan: (e, 0, 0)),
        ],
        out_specs=[spec(side), spec(parts), spec(side)],
        scratch_shapes=[pltpu.VMEM((window, DH), jnp.bfloat16)] * 6
        + [pltpu.VMEM((window, DH), jnp.float32)] * 2,
    )
    pairs = blocks * heads * window * 768
    return pl.pallas_call(
        attention_kernel,
        grid_spec=grid_spec,
        out_shape=[jax.ShapeDtypeStruct(x.shape, x.dtype) for x in (low, own, high)],
        compiler_params=pltpu.CompilerParams(vmem_limit_bytes=48 * 1024 * 1024),
        cost_estimate=pl.CostEstimate(
            flops=10 * pairs * DH,
            bytes_accessed=4 * (own.size + 2 * low.size),
            transcendentals=pairs,
        ),
    )(plan, low, own, high, row_ids, key_ids)


def from_previous(x):
    count = lax.axis_size("ctx")
    got = lax.ppermute(x, "ctx", [(i, i + 1) for i in range(count - 1)])
    wrapped = lax.ppermute(x[:-1], "ctx", [(count - 1, 0)])
    wrapped = jnp.concatenate([jnp.zeros_like(x[:1]), wrapped], axis=0)
    return jnp.where(lax.axis_index("ctx") == 0, wrapped, got)


def from_next(x):
    count = lax.axis_size("ctx")
    got = lax.ppermute(x, "ctx", [(i + 1, i) for i in range(count - 1)])
    wrapped = lax.ppermute(x[1:], "ctx", [(0, count - 1)])
    wrapped = jnp.concatenate([wrapped, jnp.zeros_like(x[:1])], axis=0)
    return jnp.where(lax.axis_index("ctx") == count - 1, wrapped, got)


def clip_plan(clip_lengths, block_rows, side_rows, enc, ctx):
    length = block_rows * enc * ctx
    window = block_rows + 2 * side_rows
    ends = jnp.cumsum(clip_lengths).astype(jnp.int32)
    starts = ends - clip_lengths
    first, last = starts // block_rows, (ends - 1) // block_rows
    edge = last * block_rows
    owner = jnp.where((first == last) | (edge - starts >= ends - edge), first, last)

    block = jnp.arange(enc, dtype=jnp.int32) * ctx + lax.axis_index("ctx")
    base = block * block_rows - side_rows
    position = base[:, None] + jnp.arange(window, dtype=jnp.int32)[None]
    inside = (position >= starts[:, None, None]) & (position < ends[:, None, None])

    def look(table):
        return jnp.sum(jnp.where(inside, table[:, None, None], 0), axis=0)

    numbers = look(jnp.arange(1, clip_lengths.shape[0] + 1, dtype=jnp.int32))
    owners = look(owner + 1) - 1
    mine = owners == block[:, None]
    row_ids = jnp.where(mine, numbers, -1)
    key_ids = jnp.where(mine, numbers, -2)
    low = jnp.where(mine, look(starts) - base[:, None], window).reshape(enc, -1, TILE).min(axis=2)
    top = jnp.where(mine, look(ends) - base[:, None], 0).reshape(enc, -1, TILE).max(axis=2)
    low = (low // ALIGN) * ALIGN
    need = top - low
    sizes = widths(window)
    kind = jnp.ones_like(need)
    chosen = jnp.full_like(need, sizes[0])
    for n in range(1, len(sizes)):
        more = need > sizes[n - 1]
        kind = jnp.where(more, n + 1, kind)
        chosen = jnp.where(more, sizes[n], chosen)
    kind = jnp.where(need > 0, kind, 0)
    low = jnp.clip(low, 0, window - chosen)
    plan = jnp.stack([low, kind], axis=1).astype(jnp.int32)
    own = owners[:, side_rows : side_rows + block_rows]
    before = own < block[:, None]
    after = own > block[:, None]
    return plan, row_ids[:, :, None], key_ids[:, None, :], before, after


def per_device(query_rows, key_rows, value_rows, out_grad, clip_lengths):
    enc, ctx, tp = (lax.axis_size(a) for a in ("enc", "ctx", "tp"))
    team = enc * tp
    rows, features = query_rows.shape
    wide = features // (team * GROUPS)
    side = tp // 2
    plan, row_ids, key_ids, before, after = clip_plan(
        clip_lengths, rows * tp, rows * side, enc, ctx
    )
    before = before.reshape(enc, tp, 1, rows, 1)[:, :side]
    after = after.reshape(enc, tp, 1, rows, 1)[:, tp - side :]
    arrays = [
        a.reshape(rows, team, GROUPS, wide) for a in (query_rows, key_rows, value_rows, out_grad)
    ]
    axes = ("enc", "tp")
    results = []
    for g in range(GROUPS):
        sent = jnp.stack([a[:, :, g].transpose(1, 0, 2) for a in arrays], axis=1)
        own = lax.all_to_all(sent, axes, split_axis=0, concat_axis=0, tiled=True)
        own = own.reshape(enc, tp, 4, rows, wide)
        low = from_previous(own[:, tp - side :])
        high = from_next(own[:, :side])
        low_out, own_out, high_out = attention(plan, low, own, high, row_ids, key_ids)
        back_low = from_previous(high_out)
        back_high = from_next(low_out)
        total = jnp.concatenate(
            [
                jnp.where(before, back_low, own_out[:, :side]),
                jnp.where(after, back_high, own_out[:, tp - side :]),
            ],
            axis=1,
        ).reshape(team, 4, rows, wide)
        results.append(lax.all_to_all(total, axes, split_axis=0, concat_axis=0, tiled=True))
    done = []
    for a in range(4):
        joined = jnp.stack([r[:, a] for r in results], axis=1)
        done.append(joined.transpose(2, 0, 1, 3).reshape(rows, features))
    return tuple(done)


def solution(mesh):
    spec = P(("enc", "ctx", "tp"), None)
    return jax.shard_map(
        per_device,
        mesh=mesh,
        in_specs=(spec, spec, spec, spec, P()),
        out_specs=(spec, spec, spec, spec),
        check_vma=False,
    )
```

```python
import functools
import math

import jax
import jax.numpy as jnp
from jax import lax
from jax.experimental import pallas as pl
from jax.experimental.pallas import tpu as pltpu
from jax.sharding import PartitionSpec as P


DH = 128
GROUPS = 3
TILE = 256
ALIGN = 128
MASKED = -1e30


def widths(window):
    steps = sorted({min(w, window) for w in (256, 512, 768, 1024, window)})
    return tuple(steps)


def attention_kernel(
    plan_ref, low_ref, own_ref, high_ref, row_ids, key_ids,
    low_out, own_out, high_out,
    q_win, k_win, v_win, g_win, out_win, dq_win, dk_win, dv_win,
):
    block = pl.program_id(0)
    rows = own_ref.shape[3]
    pieces = [(low_ref, t) for t in range(low_ref.shape[1])]
    pieces += [(own_ref, t) for t in range(own_ref.shape[1])]
    pieces += [(high_ref, t) for t in range(high_ref.shape[1])]
    window = q_win.shape[0]
    for n, (ref, t) in enumerate(pieces):
        for a, win in enumerate((q_win, k_win, v_win, g_win)):
            win[pl.ds(n * rows, rows), :] = ref[0, t, a]
    dk_win[...] = jnp.zeros_like(dk_win)
    dv_win[...] = jnp.zeros_like(dv_win)
    tiles = window // TILE
    scale = DH ** -0.5
    log_scale = scale * math.log2(math.e)

    def work(i, start, width):
        here = pl.ds(pl.multiple_of(i * TILE, TILE), TILE)
        keys = pl.ds(pl.multiple_of(start, ALIGN), width)
        q, g = q_win[here, :], g_win[here, :]
        k, v = k_win[keys, :], v_win[keys, :]
        allowed = row_ids[0, here, :] == key_ids[0, :, keys]
        across = (((1,), (1,)), ((), ()))
        down = (((0,), (0,)), ((), ()))
        s = lax.dot_general(q, k, across, preferred_element_type=jnp.float32)
        s = jnp.where(allowed, s * log_scale, MASKED)
        top = jnp.maximum(jnp.max(s, axis=1, keepdims=True), 0.1 * MASKED)
        e = jnp.exp2(s - top)
        total = jnp.sum(e, axis=1, keepdims=True)
        p = e * (1.0 / jnp.where(total > 0.0, total, 1.0))
        half = p.astype(jnp.bfloat16)
        out = jnp.dot(half, v, preferred_element_type=jnp.float32)
        correction = jnp.sum(g.astype(jnp.float32) * out, axis=1, keepdims=True)
        gp = lax.dot_general(g, v, across, preferred_element_type=jnp.float32)
        ds = (p * (gp - correction)).astype(jnp.bfloat16)
        dq = jnp.dot(ds, k, preferred_element_type=jnp.float32) * scale
        out_win[here, :] = out.astype(jnp.bfloat16)
        dq_win[here, :] = dq.astype(jnp.bfloat16)
        dk_win[keys, :] += lax.dot_general(ds, q, down, preferred_element_type=jnp.float32)
        dv_win[keys, :] += lax.dot_general(half, g, down, preferred_element_type=jnp.float32)

    def one_tile(i, carry):
        start = plan_ref[block, 0, i]
        kind = plan_ref[block, 1, i]
        for n, width in enumerate(widths(window)):
            pl.when(kind == n + 1)(functools.partial(work, i, start, width))
        return carry

    lax.fori_loop(0, tiles, one_tile, 0)
    targets = [(low_out, t) for t in range(low_ref.shape[1])]
    targets += [(own_out, t) for t in range(own_ref.shape[1])]
    targets += [(high_out, t) for t in range(high_ref.shape[1])]
    for n, (ref, t) in enumerate(targets):
        part = pl.ds(n * rows, rows)
        ref[0, t, 0] = out_win[part, :]
        ref[0, t, 1] = dq_win[part, :]
        ref[0, t, 2] = (dk_win[part, :] * scale).astype(jnp.bfloat16)
        ref[0, t, 3] = dv_win[part, :].astype(jnp.bfloat16)


def attention(plan, low, own, high, row_ids, key_ids):
    blocks, parts, arrays, rows, features = own.shape
    side = low.shape[1]
    window = (parts + 2 * side) * rows
    heads = features // DH

    def spec(count):
        return pl.BlockSpec((1, count, arrays, rows, DH), lambda e, h, plan: (e, 0, 0, 0, h))

    grid_spec = pltpu.PrefetchScalarGridSpec(
        num_scalar_prefetch=1,
        grid=(blocks, heads),
        in_specs=[
            spec(side),
            spec(parts),
            spec(side),
            pl.BlockSpec((1, window, 1), lambda e, h, plan: (e, 0, 0)),
            pl.BlockSpec((1, 1, window), lambda e, h, plan: (e, 0, 0)),
        ],
        out_specs=[spec(side), spec(parts), spec(side)],
        scratch_shapes=[pltpu.VMEM((window, DH), jnp.bfloat16)] * 6
        + [pltpu.VMEM((window, DH), jnp.float32)] * 2,
    )
    pairs = blocks * heads * window * 768
    return pl.pallas_call(
        attention_kernel,
        grid_spec=grid_spec,
        out_shape=[jax.ShapeDtypeStruct(x.shape, x.dtype) for x in (low, own, high)],
        compiler_params=pltpu.CompilerParams(vmem_limit_bytes=48 * 1024 * 1024),
        cost_estimate=pl.CostEstimate(
            flops=10 * pairs * DH,
            bytes_accessed=4 * (own.size + 2 * low.size),
            transcendentals=pairs,
        ),
    )(plan, low, own, high, row_ids, key_ids)


def from_previous(x):
    count = lax.axis_size("ctx")
    got = lax.ppermute(x, "ctx", [(i, i + 1) for i in range(count - 1)])
    wrapped = lax.ppermute(x[:-1], "ctx", [(count - 1, 0)])
    wrapped = jnp.concatenate([jnp.zeros_like(x[:1]), wrapped], axis=0)
    return jnp.where(lax.axis_index("ctx") == 0, wrapped, got)


def from_next(x):
    count = lax.axis_size("ctx")
    got = lax.ppermute(x, "ctx", [(i + 1, i) for i in range(count - 1)])
    wrapped = lax.ppermute(x[1:], "ctx", [(0, count - 1)])
    wrapped = jnp.concatenate([wrapped, jnp.zeros_like(x[:1])], axis=0)
    return jnp.where(lax.axis_index("ctx") == count - 1, wrapped, got)


def clip_plan(clip_lengths, block_rows, side_rows, enc, ctx):
    window = block_rows + 2 * side_rows
    ends = jnp.cumsum(clip_lengths).astype(jnp.int32)
    starts = ends - clip_lengths
    first, last = starts // block_rows, (ends - 1) // block_rows
    edge = last * block_rows
    owner = jnp.where((first == last) | (edge - starts >= ends - edge), first, last)

    block = jnp.arange(enc, dtype=jnp.int32) * ctx + lax.axis_index("ctx")
    base = block * block_rows - side_rows
    position = base[:, None] + jnp.arange(window, dtype=jnp.int32)[None]
    inside = (position >= starts[:, None, None]) & (position < ends[:, None, None])

    def look(table):
        return jnp.sum(jnp.where(inside, table[:, None, None], 0), axis=0)

    numbers = look(jnp.arange(1, clip_lengths.shape[0] + 1, dtype=jnp.int32))
    owners = look(owner + 1) - 1
    mine = owners == block[:, None]
    row_ids = jnp.where(mine, numbers, -1)
    key_ids = jnp.where(mine, numbers, -2)
    low = jnp.where(mine, look(starts) - base[:, None], window).reshape(enc, -1, TILE).min(axis=2)
    top = jnp.where(mine, look(ends) - base[:, None], 0).reshape(enc, -1, TILE).max(axis=2)
    low = (low // ALIGN) * ALIGN
    need = top - low
    sizes = widths(window)
    kind = jnp.ones_like(need)
    chosen = jnp.full_like(need, sizes[0])
    for n in range(1, len(sizes)):
        more = need > sizes[n - 1]
        kind = jnp.where(more, n + 1, kind)
        chosen = jnp.where(more, sizes[n], chosen)
    kind = jnp.where(need > 0, kind, 0)
    low = jnp.clip(low, 0, window - chosen)
    plan = jnp.stack([low, kind], axis=1).astype(jnp.int32)
    own = owners[:, side_rows : side_rows + block_rows]
    before = own < block[:, None]
    after = own > block[:, None]
    return plan, row_ids[:, :, None], key_ids[:, None, :], before, after


def pack_kernel(*refs):
    *arrays, packed = refs
    for a, ref in enumerate(arrays):
        packed[0, a] = ref[...]


def pack(arrays, group, team, wide):
    rows = arrays[0].shape[0]
    return pl.pallas_call(
        pack_kernel,
        grid=(team,),
        in_specs=[pl.BlockSpec((rows, wide), lambda d: (0, d * GROUPS + group))] * len(arrays),
        out_specs=pl.BlockSpec((1, len(arrays), rows, wide), lambda d: (d, 0, 0, 0)),
        out_shape=jax.ShapeDtypeStruct((team, len(arrays), rows, wide), arrays[0].dtype),
        cost_estimate=pl.CostEstimate(
            flops=0, bytes_accessed=4 * team * len(arrays) * rows * wide, transcendentals=0
        ),
    )(*arrays)


def unpack_kernel(packed, *refs):
    outs = refs[len(refs) - packed.shape[1]:]
    for a, ref in enumerate(outs):
        ref[...] = packed[0, a]


def unpack(packed, held, group):
    team, arrays, rows, wide = packed.shape
    return pl.pallas_call(
        unpack_kernel,
        grid=(team,),
        in_specs=[pl.BlockSpec((1, arrays, rows, wide), lambda d: (d, 0, 0, 0))]
        + [pl.BlockSpec(memory_space=pl.ANY)] * len(held),
        out_specs=[pl.BlockSpec((rows, wide), lambda d: (0, d * GROUPS + group))] * arrays,
        out_shape=[
            jax.ShapeDtypeStruct((rows, team * GROUPS * wide), packed.dtype)
        ] * arrays,
        input_output_aliases={1 + a: a for a in range(len(held))},
        cost_estimate=pl.CostEstimate(
            flops=0, bytes_accessed=4 * packed.size, transcendentals=0
        ),
    )(packed, *held)


def merge_kernel(side, choice, own, low, high, merged):
    t = pl.program_id(1)

    @pl.when(t < side)
    def _():
        for a in range(own.shape[2]):
            merged[0, a] = jnp.where(choice[0, 0] == 1, low[0, 0, a], own[0, 0, a])

    @pl.when(t >= side)
    def _():
        for a in range(own.shape[2]):
            merged[0, a] = jnp.where(choice[0, 0] == 2, high[0, 0, a], own[0, 0, a])


def merge(choice, own, low, high):
    enc, tp, arrays, rows, wide = own.shape
    side = low.shape[1]
    part = (1, 1, arrays, rows, wide)
    return pl.pallas_call(
        functools.partial(merge_kernel, side),
        grid=(enc, tp),
        in_specs=[
            pl.BlockSpec((1, 1, rows, 1), lambda e, t: (e, t, 0, 0)),
            pl.BlockSpec(part, lambda e, t: (e, t, 0, 0, 0)),
            pl.BlockSpec(part, lambda e, t: (e, jnp.minimum(t, side - 1), 0, 0, 0)),
            pl.BlockSpec(part, lambda e, t: (e, jnp.maximum(t - tp + side, 0), 0, 0, 0)),
        ],
        out_specs=pl.BlockSpec((1, arrays, rows, wide), lambda e, t: (e * tp + t, 0, 0, 0)),
        out_shape=jax.ShapeDtypeStruct((enc * tp, arrays, rows, wide), own.dtype),
        cost_estimate=pl.CostEstimate(
            flops=own.size, bytes_accessed=6 * own.size, transcendentals=0
        ),
    )(choice, own, low, high)


def per_device(query_rows, key_rows, value_rows, out_grad, clip_lengths):
    enc, ctx, tp = (lax.axis_size(a) for a in ("enc", "ctx", "tp"))
    team = enc * tp
    rows, features = query_rows.shape
    wide = features // (team * GROUPS)
    side = tp // 2
    arrays = (query_rows, key_rows, value_rows, out_grad)
    axes = ("enc", "tp")
    exchange = functools.partial(
        lax.all_to_all, axis_name=axes, split_axis=0, concat_axis=0, tiled=True
    )
    outs = ()
    plan, row_ids, key_ids, before, after = clip_plan(
        clip_lengths, rows * tp, rows * side, enc, ctx
    )
    choice = jnp.where(before, 1, jnp.where(after, 2, 0)).astype(jnp.int32)
    choice = choice.reshape(enc, tp, rows, 1)
    for g in range(GROUPS):
        sent = pack(arrays, g, team, wide)
        own = exchange(sent).reshape(enc, tp, 4, rows, wide)
        low = from_previous(own[:, tp - side :])
        high = from_next(own[:, :side])
        low_out, own_out, high_out = attention(plan, low, own, high, row_ids, key_ids)
        back_low = from_previous(high_out)
        back_high = from_next(low_out)
        total = merge(choice, own_out, back_low, back_high)
        total = exchange(total)
        outs = unpack(total, outs, g)
    return tuple(outs)


def solution(mesh):
    spec = P(("enc", "ctx", "tp"), None)
    return jax.shard_map(
        per_device,
        mesh=mesh,
        in_specs=(spec, spec, spec, spec, P()),
        out_specs=(spec, spec, spec, spec),
        check_vma=False,
    )
```
